32 devices in a mesh: runs: 2 (over x), gx: 16 (over z, y, core).
Axes of the slice: x: 2, y: 2, z: 4, core: 2. Of those that a mesh axis runs over, the one named last changes fastest.
Arguments:
- potential: float32 [64, 512, 512], P(('runs', 'gx')), parts along dimension 0, may hold values from -3 to 3
Outputs:
- second_potential: float32 [64, 512, 512], P(('runs', 'gx')), parts along dimension 0
- norms: float32 [4], P('runs'), parts along dimension 0
The draws below stay inside these ranges and needn't reach their ends.
There are 2 independent parts, one for each index of `runs`. The reference program is written for one: setup_inputs(seed, part) draws one part's arguments, and reference() takes and returns one part's arrays. A program takes and returns all parts, laid end to end along the dimension named above; each array names one. Nothing has to cross between parts.
All inputs are finite; a program needn't handle non-finite values.
Results may differ from the reference program's by a relative error of at most 0.00015.
Values sent between devices are 32-bit elements; how exact they have to be, the bound alone decides.
A program may use at most 256 MiB of HBM per device.

```python
import jax
import jax.numpy as jnp
from jax import lax

NY = 512
NZ = 512
LEVELS = 2
PRE = 1
POST = 1
COARSE = 4
CYCLES = 2
NX = 32


def steps_of(key, dims, split, least, high):
    level, own = 1.0, jax.random.fold_in(key, 6)
    for axis_at, parts in split:
        draws = jnp.exp(jax.random.uniform(jax.random.fold_in(own, axis_at), (parts,), jnp.float32, least / len(split), high / len(split)))
        level = level * jnp.repeat(draws, dims[axis_at] // parts).reshape([-1 if axis == axis_at else 1 for axis in range(len(dims))])
    return level


def scatter_about(stream_key, extent, width, limit, shards=(), held_as=jnp.bfloat16):
    factor_of = steps_of(stream_key, extent, shards, -0.22, 0.18) if shards else 1.0
    entries = jax.random.normal(stream_key, extent, jnp.float32) * width * factor_of
    return jnp.minimum(jnp.maximum(entries, -limit), limit).astype(held_as)


def setup_inputs(seed: int = 0, part: int = 0) -> dict:
    streams_of = jax.random.split(jax.random.key(seed), 2)
    part_splits = jax.random.split(jax.random.fold_in(streams_of[1], part), 2)
    potential = scatter_about(part_splits[0], (NX, NY, NZ), 0.5, 3.0, ((0, 16),), jnp.float32)
    return dict(potential=potential)


RELAX = 0.8

def wrap_pad(field):
    return jnp.concatenate([field[-1:], field, field[:1]], 0)

def shifted(field, offset, axis):
    return jnp.roll(field, -offset, axis)

def source_term(padded):
    center = padded[1:-1]
    upper = padded[2:]
    lower = padded[:-2]
    curve_xx = upper + lower - 2.0 * center
    curve_yy = shifted(center, 1, 1) + shifted(center, -1, 1) - 2.0 * center
    curve_zz = shifted(center, 1, 2) + shifted(center, -1, 2) - 2.0 * center
    cross_xy = (shifted(upper, 1, 1) - shifted(upper, -1, 1) - shifted(lower, 1, 1) + shifted(lower, -1, 1)) * 0.25
    cross_xz = (shifted(upper, 1, 2) - shifted(upper, -1, 2) - shifted(lower, 1, 2) + shifted(lower, -1, 2)) * 0.25
    plus_y = shifted(center, 1, 1)
    minus_y = shifted(center, -1, 1)
    cross_yz = (shifted(plus_y, 1, 2) - shifted(plus_y, -1, 2) - shifted(minus_y, 1, 2) + shifted(minus_y, -1, 2)) * 0.25
    return curve_xx * curve_yy - cross_xy * cross_xy + curve_xx * curve_zz - cross_xz * cross_xz + curve_yy * curve_zz - cross_yz * cross_yz

def operator(padded, spacing):
    center = padded[1:-1]
    beside_all = padded[2:] + padded[:-2]
    beside_all = beside_all + shifted(center, 1, 1) + shifted(center, -1, 1)
    beside_all = beside_all + shifted(center, 1, 2) + shifted(center, -1, 2)
    return (6.0 * center - beside_all) / spacing

def relax(padded, forcing, spacing):
    return padded[1:-1] + RELAX * spacing / 6.0 * (forcing - operator(padded, spacing))

def restrict(field):
    planes, rows, cols = field.shape
    blocks = field.reshape(planes // 2, 2, rows // 2, 2, cols // 2, 2)
    return lax.optimization_barrier(jnp.mean(blocks, axis=(1, 3, 5)))

def prolong(field):
    return jnp.repeat(jnp.repeat(jnp.repeat(field, 2, 0), 2, 1), 2, 2)

def smooth(field, forcing, spacing, count):
    for sweep_index in range(count):
        field = relax(wrap_pad(field), forcing, spacing)
    return field

def vcycle(field, forcing, level):
    spacing = float(4 ** level)
    if level == LEVELS - 1:
        return smooth(jnp.zeros_like(forcing), forcing, spacing, COARSE)
    field = smooth(field, forcing, spacing, PRE)
    residue = forcing - operator(wrap_pad(field), spacing)
    coarse_rhs = restrict(residue)
    correction = vcycle(jnp.zeros_like(coarse_rhs), coarse_rhs, level + 1)
    field = field + prolong(correction)
    return smooth(field, forcing, spacing, POST)

def reference(potential):
    source = source_term(wrap_pad(potential))
    forcing = -(source - jnp.mean(source))
    field = jnp.zeros_like(forcing)
    results = []
    for cycle_index in range(CYCLES):
        field = vcycle(field, forcing, 0)
        residue = forcing - operator(wrap_pad(field), 1.0)
        results.append(jnp.sqrt(jnp.mean(residue * residue)))
    return (field, jnp.stack(results))
```

```python
import functools

import jax
import jax.numpy as jnp
from jax import lax
from jax.experimental import pallas as pl
from jax.experimental.pallas import tpu as pltpu
from jax.sharding import PartitionSpec as P

GROUP = 4
HX = 5
HY = 24
PAD = 8
CH = 16
A = 0.8 / 6.0
F32 = jnp.float32
BF16 = jnp.bfloat16


def split_dot(x, m):
    hi = x.astype(BF16)
    lo = (x - hi.astype(F32)).astype(BF16)
    return jnp.dot(hi, m, preferred_element_type=F32) + jnp.dot(lo, m, preferred_element_type=F32)


def dot_split(m, x):
    hi = x.astype(BF16)
    lo = (x - hi.astype(F32)).astype(BF16)
    return jnp.dot(m, hi, preferred_element_type=F32) + jnp.dot(m, lo, preferred_element_type=F32)


def kernel(
    n, p_ref, o_ref, nrm_ref,
    pv, fv, wv, tmp, c1, c2, ea, eb, sbuf, nbuf, rmat, tmat, lmat, umat,
    in_send, in_recv, halo_send, halo_recv, c_send, c_recv, s_send, s_recv, n_send, n_recv,
    out_send, out_recv, local_sem,
):
    planes, ny, nz = p_ref.shape
    rows = ny // GROUP
    R = rows + 2 * HY
    own = planes * GROUP
    co = own // 2
    total = own + 2 * HX
    cells = float(n * planes * ny * nz)
    me = lax.axis_index("gx")
    member = lax.rem(me, GROUP)
    base = me - member
    right = lax.rem(me + GROUP, n)
    left = lax.rem(me + n - GROUP, n)

    barrier = pltpu.get_barrier_semaphore()

    def greet(k, _):
        pl.semaphore_signal(barrier, inc=1, device_id={"gx": lax.rem(me + k, n)})
        return 0

    lax.fori_loop(1, n, greet, 0)
    pl.semaphore_wait(barrier, n - 1)

    def pieces(t):
        first = t * rows
        return (
            (first, PAD + HY, rows),
            (lax.rem(first + ny - HY, ny), PAD, HY),
            (lax.rem(first + rows, ny), PAD + HY + rows, HY),
        )

    def in_copy(step, piece, start, at, size):
        src = p_ref.at[:, pl.ds(pl.multiple_of(start, 8), size), :]
        dst = pv.at[pl.ds(HX + planes * member, planes), pl.ds(at, size), :]
        if step == 0:
            return pltpu.make_async_copy(src, dst, local_sem.at[piece])
        return pltpu.make_async_remote_copy(
            src, dst, in_send.at[step, piece], in_recv.at[step, piece],
            device_id={"gx": base + lax.rem(member + step, GROUP)},
        )

    sends = []
    for step in (1, 2, 3, 0):
        t = lax.rem(member + step, GROUP)
        for piece, (start, at, size) in enumerate(pieces(t)):
            copy = in_copy(step, piece, start, at, size)
            copy.start()
            sends.append(copy)

    zeros = jnp.zeros((PAD, nz), F32)
    for ref in (pv, fv, wv):
        def clear(i, _, ref=ref):
            ref[i, 0:PAD, :] = zeros
            ref[i, PAD + R : 2 * PAD + R, :] = zeros
            return 0
        lax.fori_loop(0, total, clear, 0)

    def pairs(shape, fine):
        idx = lax.broadcasted_iota(jnp.int32, shape, fine)
        other = lax.broadcasted_iota(jnp.int32, shape, 1 - fine)
        return jnp.where(idx // 2 == other, 1.0, 0.0).astype(BF16)

    rmat[...] = pairs(rmat.shape, 0)
    tmat[...] = pairs(tmat.shape, 1)
    lmat[...] = pairs(lmat.shape, 1)
    umat[...] = pairs(umat.shape, 0)

    for copy in sends:
        copy.wait()

    batch = ((own - 2, 2), (own - 4, 2), (own - 5, 1))
    halos = []
    for b, (at, size) in enumerate(batch):
        halos.append(pltpu.make_async_remote_copy(
            pv.at[pl.ds(HX + at, size), pl.ds(PAD, R), :],
            pv.at[pl.ds(HX + at - own, size), pl.ds(PAD, R), :],
            halo_send.at[0, b], halo_recv.at[0, b], device_id={"gx": right}))
        low = own - at - size
        halos.append(pltpu.make_async_remote_copy(
            pv.at[pl.ds(HX + low, size), pl.ds(PAD, R), :],
            pv.at[pl.ds(HX + own + low, size), pl.ds(PAD, R), :],
            halo_send.at[1, b], halo_recv.at[1, b], device_id={"gx": left}))
    for copy in halos:
        copy.start()
    for copy in halos:
        copy.wait()

    chunks = R // CH

    def at_row(k):
        return pl.multiple_of(PAD + k * CH, 8)

    def window(ref, i, r0):
        return ref[i, pl.ds(pl.multiple_of(r0 - 8, 8), CH + 16), :]

    def up(w):
        return pltpu.roll(w, CH + 15, 0)[8 : 8 + CH]

    def down(w):
        return pltpu.roll(w, 1, 0)[8 : 8 + CH]

    def zp(x):
        return pltpu.roll(x, nz - 1, 1)

    def zm(x):
        return pltpu.roll(x, 1, 1)

    def beside(ref, i, r0):
        w = window(ref, i, r0)
        c = w[8 : 8 + CH]
        s = ref[i - 1, pl.ds(r0, CH), :] + ref[i + 1, pl.ds(r0, CH), :]
        return c, s + (up(w) + down(w)) + (zp(c) + zm(c))

    def own_rows(r0, x):
        row = lax.broadcasted_iota(jnp.int32, (CH, nz), 0) + r0
        return jnp.where((row >= PAD + HY) & (row < PAD + HY + rows), x, 0.0)

    def fold(x):
        t = x[0:8]
        for k in range(1, CH // 8):
            t = t + x[8 * k : 8 * k + 8]
        u = t[:, 0:128]
        for k in range(1, nz // 128):
            u = u + t[:, 128 * k : 128 * k + 128]
        return u

    def over(lo, hi, body, acc=0):
        def plane(i, acc):
            def chunk(k, acc):
                return body(i, at_row(k), acc)
            return lax.fori_loop(0, chunks, chunk, acc)
        return lax.fori_loop(lo, hi, plane, acc)

    acc0 = jnp.zeros((8, 128), F32)

    def source(i, r0):
        w = window(pv, i, r0)
        u = window(pv, i + 1, r0)
        l = window(pv, i - 1, r0)
        c = w[8 : 8 + CH]
        cu, cd = up(w), down(w)
        c2x = 2.0 * c
        xx = u[8 : 8 + CH] + l[8 : 8 + CH] - c2x
        yy = cu + cd - c2x
        zz = zp(c) + zm(c) - c2x
        d = u - l
        xy = up(d) - down(d)
        dc = d[8 : 8 + CH]
        xz = zp(dc) - zm(dc)
        g = cu - cd
        yz = zp(g) - zm(g)
        return xx * yy + (xx + yy) * zz - 0.0625 * (xy * xy + xz * xz + yz * yz)

    def source_body(i, r0, acc):
        s = source(i, r0)
        fv[i, pl.ds(r0, CH), :] = -s
        return acc

    def source_own(i, r0, acc):
        s = source(i, r0)
        fv[i, pl.ds(r0, CH), :] = -s
        return acc + fold(own_rows(r0, s))

    acc = over(HX, HX + own, source_own, acc0)

    def share(buf, send, recv, k):
        return pltpu.make_async_remote_copy(
            buf.at[0], buf.at[k], send.at[k], recv.at[k],
            device_id={"gx": lax.rem(me + k, n)})

    def share_start(buf, send, recv):
        def go(k, _):
            share(buf, send, recv, k).start()
            return 0
        lax.fori_loop(1, n, go, 0)

    def share_wait(buf, send, recv):
        def go(k, _):
            share(buf, send, recv, k).wait()
            return 0
        lax.fori_loop(1, n, go, 0)
        return lax.fori_loop(1, n, lambda k, t: t + buf[k], buf[0])

    sbuf[0] = acc
    over(1, HX, source_body)
    over(HX + own, total - 1, source_body)
    share_start(sbuf, s_send, s_recv)

    def restrict_into(c, lo, hi, residual):
        def plane(j, _):
            i = HX + 2 * (j - 5)
            def chunk(k, _):
                r0 = at_row(k)
                tmp[pl.ds(pl.multiple_of(k * CH, 8), CH), :] = residual(i, r0) + residual(i + 1, r0)
                return 0
            lax.fori_loop(0, chunks, chunk, 0)
            half = dot_split(lmat[...], tmp[...])
            c[j] = split_dot(half, rmat[...]) * 0.125
            return 0
        lax.fori_loop(lo, hi, plane, 0)

    def residual_first(i, r0):
        c, s = beside(fv, i, r0)
        return c - A * (6.0 * c - s)

    restrict_into(c1, 4, 6 + co, residual_first)

    def coarse_trade(c, to_right, at_right, to_left, at_left, slot):
        copies = (
            pltpu.make_async_remote_copy(
                c.at[pl.ds(to_right, 4)], c.at[pl.ds(at_right, 4)],
                c_send.at[slot, 0], c_recv.at[slot, 0], device_id={"gx": right}),
            pltpu.make_async_remote_copy(
                c.at[pl.ds(to_left, 4)], c.at[pl.ds(at_left, 4)],
                c_send.at[slot, 1], c_recv.at[slot, 1], device_id={"gx": left}),
        )
        for copy in copies:
            copy.start()
        for copy in copies:
            copy.wait()

    coarse_trade(c1, co, 0, 6, 6 + co, 0)
    mean = jnp.sum(share_wait(sbuf, s_send, s_recv)) / cells

    cr, cc = c1.shape[1:]

    def coarse_solve(c, lo, hi, shift):
        def first(j, _):
            f = (c[j] + shift) * 4.0
            c[j] = f
            ea[j] = A * f
            return 0
        lax.fori_loop(lo, hi, first, 0)
        src, dst = ea, eb
        for sweep in range(1, 4):
            def again(j, _, src=src, dst=dst):
                v = src[j]
                s = src[j - 1] + src[j + 1]
                s = s + pltpu.roll(v, 1, 0) + pltpu.roll(v, cr - 1, 0)
                s = s + pltpu.roll(v, 1, 1) + pltpu.roll(v, cc - 1, 1)
                dst[j] = 0.2 * v + A * (c[j] + s)
                return 0
            lax.fori_loop(lo + sweep, hi - sweep, again, 0)
            src, dst = dst, src
        return src

    def prolonged(e, j):
        x = e[j]
        return dot_split(umat[...], split_dot(x, tmat[...]))

    e1 = coarse_solve(c1, 0, 10 + co, mean)

    def add_first(j, _):
        tmp[...] = prolonged(e1, j)
        i = HX + 2 * (j - 5)
        def chunk(k, _):
            r0 = at_row(k)
            x = tmp[pl.ds(pl.multiple_of(k * CH, 8), CH), :]
            for q in range(2):
                f = fv[i + q, pl.ds(r0, CH), :] + mean
                fv[i + q, pl.ds(r0, CH), :] = f
                pv[i + q, pl.ds(r0, CH), :] = A * f + x
            return 0
        lax.fori_loop(0, chunks, chunk, 0)
        return 0

    lax.fori_loop(3, 7 + co, add_first, 0)

    def relax_body(src, dst):
        def body(i, r0, acc):
            c, s = beside(src, i, r0)
            dst[i, pl.ds(r0, CH), :] = 0.2 * c + A * (fv[i, pl.ds(r0, CH), :] + s)
            return acc
        return body

    over(2, total - 2, relax_body(pv, wv))

    def relax_norm(i, r0, acc):
        c, s = beside(wv, i, r0)
        r = fv[i, pl.ds(r0, CH), :] - (6.0 * c - s)
        pv[i, pl.ds(r0, CH), :] = c + A * r
        return acc + fold(own_rows(r0, r * r))

    over(3, HX, relax_body(wv, pv))
    norm1 = over(HX, HX + own, relax_norm, acc0)
    over(HX + own, total - 3, relax_body(wv, pv))

    def residual_second(i, r0):
        c, s = beside(pv, i, r0)
        return fv[i, pl.ds(r0, CH), :] - (6.0 * c - s)

    restrict_into(c2, 5, 5 + co, residual_second)
    coarse_trade(c2, 1 + co, 1, 5, 5 + co, 1)
    e2 = coarse_solve(c2, 1, 9 + co, 0.0)

    def add_second(j, _):
        tmp[...] = prolonged(e2, j)
        i = HX + 2 * (j - 5)
        def chunk(k, _):
            r0 = at_row(k)
            x = tmp[pl.ds(pl.multiple_of(k * CH, 8), CH), :]
            for q in range(2):
                pv[i + q, pl.ds(r0, CH), :] = pv[i + q, pl.ds(r0, CH), :] + x
            return 0
        lax.fori_loop(0, chunks, chunk, 0)
        return 0

    lax.fori_loop(4, 6 + co, add_second, 0)
    over(4, total - 4, relax_body(pv, wv))

    def out_copy(step):
        t = lax.rem(member + step, GROUP)
        src = wv.at[pl.ds(HX + planes * t, planes), pl.ds(PAD + HY, rows), :]
        dst = o_ref.at[:, pl.ds(pl.multiple_of(member * rows, 8), rows), :]
        if step == 0:
            return pltpu.make_async_copy(src, dst, local_sem.at[3])
        return pltpu.make_async_remote_copy(
            src, dst, out_send.at[step], out_recv.at[step], device_id={"gx": base + t})

    outs = [out_copy(step) for step in (1, 2, 3, 0)]
    for copy in outs:
        copy.start()

    def norm_body(i, r0, acc):
        c, s = beside(wv, i, r0)
        r = fv[i, pl.ds(r0, CH), :] - (6.0 * c - s)
        return acc + fold(own_rows(r0, r * r))

    norm2 = over(HX, HX + own, norm_body, acc0)
    nbuf[0, 0:8, :] = norm1
    nbuf[0, 8:16, :] = norm2
    share_start(nbuf, n_send, n_recv)
    sums = share_wait(nbuf, n_send, n_recv)
    nrm_ref[0:8, :] = jnp.sqrt(jnp.full((8, 128), jnp.sum(sums[0:8]) / cells, F32))
    nrm_ref[8:16, :] = jnp.sqrt(jnp.full((8, 128), jnp.sum(sums[8:16]) / cells, F32))
    for copy in outs:
        copy.wait()


def on_device(n, potential):
    planes, ny, nz = potential.shape
    R = ny // GROUP + 2 * HY
    total = planes * GROUP + 2 * HX
    coarse = planes * GROUP // 2 + 10
    fine = pltpu.VMEM((total, R + 2 * PAD, nz), F32)
    small = pltpu.VMEM((coarse, R // 2, nz // 2), F32)
    dma = pltpu.SemaphoreType.DMA
    field, norms = pl.pallas_call(
        functools.partial(kernel, n),
        out_shape=(
            jax.ShapeDtypeStruct(potential.shape, F32),
            jax.ShapeDtypeStruct((16, 128), F32),
        ),
        in_specs=[pl.BlockSpec(memory_space=pl.ANY)],
        out_specs=(pl.BlockSpec(memory_space=pl.ANY), pl.BlockSpec(memory_space=pltpu.VMEM)),
        scratch_shapes=[
            fine, fine, fine, pltpu.VMEM((R, nz), F32), small, small, small, small,
            pltpu.VMEM((n, 8, 128), F32), pltpu.VMEM((n, 16, 128), F32),
            pltpu.VMEM((nz, nz // 2), BF16), pltpu.VMEM((nz // 2, nz), BF16),
            pltpu.VMEM((R // 2, R), BF16), pltpu.VMEM((R, R // 2), BF16),
            dma((4, 3)), dma((4, 3)), dma((2, 3)), dma((2, 3)), dma((2, 2)), dma((2, 2)),
            dma((n,)), dma((n,)), dma((n,)), dma((n,)), dma((4,)), dma((4,)), dma((4,)),
        ],
        compiler_params=pltpu.CompilerParams(
            collective_id=0, has_side_effects=True, vmem_limit_bytes=60 << 20),
        name="vcycles",
    )(potential)
    return field, jnp.stack([norms[0, 0], norms[8, 0]])


def solution(mesh):
    n = mesh.shape["gx"]
    return jax.shard_map(
        functools.partial(on_device, n),
        mesh=mesh,
        in_specs=P(("runs", "gx"), None, None),
        out_specs=(P(("runs", "gx"), None, None), P("runs")),
        check_vma=False,
    )
```

```python
import functools

import jax
import jax.numpy as jnp
from jax import lax
from jax.experimental import pallas as pl
from jax.experimental.pallas import tpu as pltpu
from jax.sharding import PartitionSpec as P

HY = 24
PAD = 8
A = 0.8 / 6.0
F32 = jnp.float32
BF16 = jnp.bfloat16


def split_dot(x, m):
    hi = x.astype(BF16)
    lo = (x - hi.astype(F32)).astype(BF16)
    return jnp.dot(hi, m, preferred_element_type=F32) + jnp.dot(lo, m, preferred_element_type=F32)


def dot_split(m, x):
    hi = x.astype(BF16)
    lo = (x - hi.astype(F32)).astype(BF16)
    return jnp.dot(m, hi, preferred_element_type=F32) + jnp.dot(m, lo, preferred_element_type=F32)


def kernel(
    n, p_ref, o_ref, nrm_ref,
    pv, fv, wv, tmp, cf, ea, eb, sbuf, nbuf, rmat, tmat, lmat, umat,
    in_send, in_recv, halo_send, halo_recv, s_send, s_recv, n_send, n_recv,
    out_send, out_recv, local_sem,
):
    planes, ny, nz = p_ref.shape
    rows = ny // n
    R = rows + 2 * HY
    blocks = R // 8
    nx = planes * n
    half = nx // 2
    cells = float(nx * ny * nz)
    chips = n // 2
    me = lax.axis_index("gx")

    def ring_of(d):
        chip = d // 2
        odd = chip % 2
        pos = (1 - odd) * (chip // 2) + odd * (chips - 1 - chip // 2)
        return 2 * pos + d % 2

    def device_at(r):
        pos = r // 2
        back = pos // (chips // 2)
        chip = (1 - back) * (2 * pos) + back * (2 * (chips - 1 - pos) + 1)
        return 2 * chip + r % 2

    def partner(k):
        t = 0
        bit = 1
        while bit < n:
            t = t + (((me // bit) % 2 + (k // bit) % 2) % 2) * bit
            bit *= 2
        return t

    here = ring_of(me)

    barrier = pltpu.get_barrier_semaphore()

    def greet(k, _):
        pl.semaphore_signal(barrier, inc=1, device_id={"gx": lax.rem(me + k, n)})
        return 0

    lax.fori_loop(1, n, greet, 0)
    pl.semaphore_wait(barrier, n - 1)

    def in_copy(k):
        t = partner(k)
        src = p_ref.at[:, pl.ds(pl.multiple_of(ring_of(t) * rows, 8), rows), :]
        dst = pv.at[pl.ds(planes * me, planes), pl.ds(PAD + HY, rows), :]
        if k == 0:
            return pltpu.make_async_copy(src, dst, local_sem.at[0])
        return pltpu.make_async_remote_copy(
            src, dst, in_send.at[k], in_recv.at[k], device_id={"gx": t})

    ins = [in_copy(k) for k in range(n)]
    for k in range(n - 1, -1, -1):
        ins[k].start()

    zeros = jnp.zeros((PAD, nz), F32)

    def clear(i, _):
        for ref in (pv, fv, wv):
            ref[i, 0:PAD, :] = zeros
            ref[i, PAD + R : 2 * PAD + R, :] = zeros
        return 0

    lax.fori_loop(0, nx, clear, 0)

    def pairs(shape, fine):
        idx = lax.broadcasted_iota(jnp.int32, shape, fine)
        other = lax.broadcasted_iota(jnp.int32, shape, 1 - fine)
        return jnp.where(idx // 2 == other, 1.0, 0.0).astype(BF16)

    rmat[...] = pairs(rmat.shape, 0)
    tmat[...] = pairs(tmat.shape, 1)
    lmat[...] = pairs(lmat.shape, 1)
    umat[...] = pairs(umat.shape, 0)

    def halo_copies(b, start):
        copies = []
        at = PAD + HY
        for h in range((HY + rows - 1) // rows):
            size = min(rows, HY - h * rows)
            span = pl.ds(start, half)
            copies.append(pltpu.make_async_remote_copy(
                pv.at[span, pl.ds(at + rows - size, size), :],
                pv.at[span, pl.ds(at - h * rows - size, size), :],
                halo_send.at[b, 0, h], halo_recv.at[b, 0, h],
                device_id={"gx": device_at((here + 1 + h) % n)}))
            copies.append(pltpu.make_async_remote_copy(
                pv.at[span, pl.ds(at, size), :],
                pv.at[span, pl.ds(at + rows + h * rows, size), :],
                halo_send.at[b, 1, h], halo_recv.at[b, 1, h],
                device_id={"gx": device_at((here + n - 1 - h) % n)}))
        return copies

    mine = me // (n // 2)
    far = (1 - mine) * half
    near = mine * half
    for k in range(n - 1, n // 2 - 1, -1):
        ins[k].wait()
    halos = halo_copies(0, far)
    for copy in halos:
        copy.start()
    for k in range(n // 2 - 1, -1, -1):
        ins[k].wait()
    more = halo_copies(1, near)
    for copy in more:
        copy.start()
    for copy in halos + more:
        copy.wait()

    def spans(lo, hi):
        out = []
        while lo < hi:
            size = min(2, hi - lo)
            out.append((PAD + 8 * lo, 8 * size))
            lo += size
        return out

    def before(i):
        return lax.rem(i + nx - 1, nx)

    def after(i):
        return lax.rem(i + 1, nx)

    def zp(x):
        return pltpu.roll(x, nz - 1, 1)

    def zm(x):
        return pltpu.roll(x, 1, 1)

    def beside(ref, i, r, size):
        c = ref[i, r : r + size, :]
        s = ref[before(i), r : r + size, :] + ref[after(i), r : r + size, :]
        y = ref[i, r - 1 : r - 1 + size, :] + ref[i, r + 1 : r + 1 + size, :]
        return c, s + y + (zp(c) + zm(c))

    def fold(x):
        t = x[0:8]
        for k in range(1, x.shape[0] // 8):
            t = t + x[8 * k : 8 * k + 8]
        u = t[:, 0:128]
        for k in range(1, nz // 128):
            u = u + t[:, 128 * k : 128 * k + 128]
        return u

    def over(lo, hi, body, acc=0, start=0, count=nx):
        def plane(i, acc):
            for r, size in spans(lo, hi):
                acc = body(i, r, size, acc)
            return acc
        return lax.fori_loop(start, start + count, plane, acc)

    own = (HY // 8, blocks - HY // 8)
    acc0 = jnp.zeros((8, 128), F32)

    def source(i, r, size):
        lower, upper = before(i), after(i)
        def at(k, q):
            return pv[k, r + q : r + q + size, :]
        c, cu, cd = at(i, 0), at(i, 1), at(i, -1)
        u, l = at(upper, 0), at(lower, 0)
        c2x = 2.0 * c
        xx = u + l - c2x
        yy = cu + cd - c2x
        zz = zp(c) + zm(c) - c2x
        xy = (at(upper, 1) - at(lower, 1)) - (at(upper, -1) - at(lower, -1))
        d = u - l
        xz = zp(d) - zm(d)
        g = cu - cd
        yz = zp(g) - zm(g)
        return xx * yy + (xx + yy) * zz - 0.0625 * (xy * xy + xz * xz + yz * yz)

    def source_plane(i, acc):
        for lo, hi in ((0, own[0]), own, (own[1], blocks)):
            for r, size in spans(lo, hi):
                s = source(i, r, size)
                fv[i, r : r + size, :] = -s
                if (lo, hi) == own:
                    acc = acc + fold(s)
        return acc

    sbuf[0] = lax.fori_loop(0, nx, source_plane, acc0)

    def share(buf, send, recv, k):
        return pltpu.make_async_remote_copy(
            buf.at[0], buf.at[k], send.at[k], recv.at[k],
            device_id={"gx": lax.rem(me + k, n)})

    def share_start(buf, send, recv):
        def go(k, _):
            share(buf, send, recv, k).start()
            return 0
        lax.fori_loop(1, n, go, 0)

    def share_wait(buf, send, recv):
        def go(k, _):
            share(buf, send, recv, k).wait()
            return 0
        lax.fori_loop(1, n, go, 0)
        return lax.fori_loop(1, n, lambda k, t: t + buf[k], buf[0])

    share_start(sbuf, s_send, s_recv)

    def restrict(lo, hi, residual):
        def plane(j, _):
            for r, size in spans(lo, hi):
                tmp[r - PAD : r - PAD + size, :] = residual(2 * j, r, size) + residual(2 * j + 1, r, size)
            cf[j] = split_dot(dot_split(lmat[...], tmp[...]), rmat[...]) * 0.125
            return 0
        lax.fori_loop(0, half, plane, 0)

    def residual_first(i, r, size):
        c, s = beside(fv, i, r, size)
        return c - A * (6.0 * c - s)

    restrict(0, blocks, residual_first)
    mean = jnp.sum(share_wait(sbuf, s_send, s_recv)) / cells

    cr, cc = cf.shape[1:]

    def coarse_solve(shift):
        def first(j, _):
            f = (cf[j] + shift) * 4.0
            cf[j] = f
            ea[j] = A * f
            return 0
        lax.fori_loop(0, half, first, 0)
        src, dst = ea, eb
        for sweep in range(3):
            def again(j, _, src=src, dst=dst):
                v = src[j]
                s = src[lax.rem(j + half - 1, half)] + src[lax.rem(j + 1, half)]
                s = s + pltpu.roll(v, 1, 0) + pltpu.roll(v, cr - 1, 0)
                s = s + pltpu.roll(v, 1, 1) + pltpu.roll(v, cc - 1, 1)
                dst[j] = 0.2 * v + A * (cf[j] + s)
                return 0
            lax.fori_loop(0, half, again, 0)
            src, dst = dst, src
        return src

    def prolong(e, lo, hi, add):
        def plane(j, _):
            tmp[...] = dot_split(umat[...], split_dot(e[j], tmat[...]))
            for r, size in spans(lo, hi):
                x = tmp[r - PAD : r - PAD + size, :]
                for q in range(2):
                    add(2 * j + q, r, size, x)
            return 0
        lax.fori_loop(0, half, plane, 0)

    def add_first(i, r, size, x):
        f = fv[i, r : r + size, :] + mean
        fv[i, r : r + size, :] = f
        pv[i, r : r + size, :] = A * f + x

    def add_second(i, r, size, x):
        pv[i, r : r + size, :] = pv[i, r : r + size, :] + x

    def relax(i, r, size, acc):
        c, s = beside(pv, i, r, size)
        wv[i, r : r + size, :] = 0.2 * c + A * (fv[i, r : r + size, :] + s)
        return acc

    def residual_of(ref, i, r, size):
        c, s = beside(ref, i, r, size)
        return c, fv[i, r : r + size, :] - (6.0 * c - s)

    def relax_norm(i, acc):
        for lo, hi in ((1, own[0]), own, (own[1], blocks - 1)):
            for r, size in spans(lo, hi):
                c, res = residual_of(wv, i, r, size)
                pv[i, r : r + size, :] = c + A * res
                if (lo, hi) == own:
                    acc = acc + fold(res * res)
        return acc

    prolong(coarse_solve(mean), 1, blocks - 1, add_first)
    over(1, blocks - 1, relax)
    nbuf[0, 0:8, :] = lax.fori_loop(0, nx, relax_norm, acc0)

    restrict(2, blocks - 2, lambda i, r, size: residual_of(pv, i, r, size)[1])
    prolong(coarse_solve(0.0), 2, blocks - 2, add_second)

    def out_copy(k):
        t = partner(k)
        src = wv.at[pl.ds(planes * t, planes), pl.ds(PAD + HY, rows), :]
        dst = o_ref.at[:, pl.ds(pl.multiple_of(here * rows, 8), rows), :]
        if k == 0:
            return pltpu.make_async_copy(src, dst, local_sem.at[1])
        return pltpu.make_async_remote_copy(
            src, dst, out_send.at[k], out_recv.at[k], device_id={"gx": t})

    outs = [out_copy(k) for k in range(n)]
    over(2, blocks - 2, relax, start=far, count=half)
    for k in range(n - 1, n // 2 - 1, -1):
        outs[k].start()
    over(2, blocks - 2, relax, start=near, count=half)
    for k in range(n // 2 - 1, -1, -1):
        outs[k].start()

    def norm_body(i, r, size, acc):
        res = residual_of(wv, i, r, size)[1]
        return acc + fold(res * res)

    nbuf[0, 8:16, :] = over(*own, norm_body, acc0)
    share_start(nbuf, n_send, n_recv)
    sums = share_wait(nbuf, n_send, n_recv)
    nrm_ref[0:8, :] = jnp.sqrt(jnp.full((8, 128), jnp.sum(sums[0:8]) / cells, F32))
    nrm_ref[8:16, :] = jnp.sqrt(jnp.full((8, 128), jnp.sum(sums[8:16]) / cells, F32))
    for copy in outs:
        copy.wait()


def on_device(n, potential):
    planes, ny, nz = potential.shape
    R = ny // n + 2 * HY
    nx = planes * n
    cr = (R // 2 + 7) // 8 * 8
    hops = -(-HY // (ny // n))
    fine = pltpu.VMEM((nx, R + 2 * PAD, nz), F32)
    small = pltpu.VMEM((nx // 2, cr, nz // 2), F32)
    dma = pltpu.SemaphoreType.DMA
    field, norms = pl.pallas_call(
        functools.partial(kernel, n),
        out_shape=(
            jax.ShapeDtypeStruct(potential.shape, F32),
            jax.ShapeDtypeStruct((16, 128), F32),
        ),
        in_specs=[pl.BlockSpec(memory_space=pl.ANY)],
        out_specs=(pl.BlockSpec(memory_space=pl.ANY), pl.BlockSpec(memory_space=pltpu.VMEM)),
        scratch_shapes=[
            fine, fine, fine, pltpu.VMEM((R, nz), F32), small, small, small,
            pltpu.VMEM((n, 8, 128), F32), pltpu.VMEM((n, 16, 128), F32),
            pltpu.VMEM((nz, nz // 2), BF16), pltpu.VMEM((nz // 2, nz), BF16),
            pltpu.VMEM((cr, R), BF16), pltpu.VMEM((R, cr), BF16),
            dma((n,)), dma((n,)), dma((2, 2, hops)), dma((2, 2, hops)),
            dma((n,)), dma((n,)), dma((n,)), dma((n,)), dma((n,)), dma((n,)), dma((2,)),
        ],
        compiler_params=pltpu.CompilerParams(
            collective_id=0, has_side_effects=True, vmem_limit_bytes=67043328),
        name="vcycles",
    )(potential)
    return field, jnp.stack([norms[0, 0], norms[8, 0]])


def solution(mesh):
    n = mesh.shape["gx"]
    return jax.shard_map(
        functools.partial(on_device, n),
        mesh=mesh,
        in_specs=P(("runs", "gx"), None, None),
        out_specs=(P(("runs", "gx"), None, None), P("runs")),
        check_vma=False,
    )
```

```python
import functools

import jax
import jax.numpy as jnp
from jax import lax
from jax.experimental import pallas as pl
from jax.experimental.pallas import tpu as pltpu
from jax.sharding import PartitionSpec as P

HY = 24
PAD = 8
A = 0.8 / 6.0
F32 = jnp.float32
BF16 = jnp.bfloat16


def split_dot(x, m):
    hi = x.astype(BF16)
    lo = (x - hi.astype(F32)).astype(BF16)
    return jnp.dot(hi, m, preferred_element_type=F32) + jnp.dot(lo, m, preferred_element_type=F32)


def kernel(
    n, p_ref, o_ref, nrm_ref,
    pv, fv, wv, tmp, cf, ea, eb, sbuf, nbuf, rmat, tmat,
    in_send, in_recv, halo_send, halo_recv, s_send, s_recv, n_send, n_recv,
    out_send, out_recv, local_sem,
):
    planes, ny, nz = p_ref.shape
    rows = ny // n
    R = rows + 2 * HY
    blocks = R // 8
    nx = planes * n
    half = nx // 2
    cells = float(nx * ny * nz)
    chips = n // 2
    me = lax.axis_index("gx")

    def ring_of(d):
        chip = d // 2
        odd = chip % 2
        pos = (1 - odd) * (chip // 2) + odd * (chips - 1 - chip // 2)
        return 2 * pos + d % 2

    def device_at(r):
        pos = r // 2
        back = pos // (chips // 2)
        chip = (1 - back) * (2 * pos) + back * (2 * (chips - 1 - pos) + 1)
        return 2 * chip + r % 2

    def partner(k):
        t = 0
        bit = 1
        while bit < n:
            t = t + (((me // bit) % 2 + (k // bit) % 2) % 2) * bit
            bit *= 2
        return t

    here = ring_of(me)

    barrier = pltpu.get_barrier_semaphore()

    def greet(k, _):
        pl.semaphore_signal(barrier, inc=1, device_id={"gx": lax.rem(me + k, n)})
        return 0

    lax.fori_loop(1, n, greet, 0)
    pl.semaphore_wait(barrier, n - 1)

    def in_copy(k):
        t = partner(k)
        src = p_ref.at[:, pl.ds(pl.multiple_of(ring_of(t) * rows, 8), rows), :]
        dst = pv.at[pl.ds(planes * me, planes), pl.ds(PAD + HY, rows), :]
        if k == 0:
            return pltpu.make_async_copy(src, dst, local_sem.at[0])
        return pltpu.make_async_remote_copy(
            src, dst, in_send.at[k], in_recv.at[k], device_id={"gx": t})

    ins = [in_copy(k) for k in range(n)]
    quarter = n // 4
    for k in range(quarter):
        for q in (3, 1, 2, 0):
            ins[q * quarter + k].start()

    zeros = jnp.zeros((PAD, nz), F32)

    def clear(i, _):
        for ref in (pv, fv, wv):
            ref[i, 0:PAD, :] = zeros
            ref[i, PAD + R : 2 * PAD + R, :] = zeros
        return 0

    lax.fori_loop(0, nx, clear, 0)

    def pairs(shape, fine):
        idx = lax.broadcasted_iota(jnp.int32, shape, fine)
        other = lax.broadcasted_iota(jnp.int32, shape, 1 - fine)
        return jnp.where(idx // 2 == other, 1.0, 0.0).astype(BF16)

    rmat[...] = pairs(rmat.shape, 0)
    tmat[...] = pairs(tmat.shape, 1)

    def halo_copies(b, start):
        copies = []
        at = PAD + HY
        for h in range((HY + rows - 1) // rows):
            size = min(rows, HY - h * rows)
            span = pl.ds(start, nx // 4)
            copies.append(pltpu.make_async_remote_copy(
                pv.at[span, pl.ds(at + rows - size, size), :],
                pv.at[span, pl.ds(at - h * rows - size, size), :],
                halo_send.at[b, 0, h], halo_recv.at[b, 0, h],
                device_id={"gx": device_at((here + 1 + h) % n)}))
            copies.append(pltpu.make_async_remote_copy(
                pv.at[span, pl.ds(at, size), :],
                pv.at[span, pl.ds(at + rows + h * rows, size), :],
                halo_send.at[b, 1, h], halo_recv.at[b, 1, h],
                device_id={"gx": device_at((here + n - 1 - h) % n)}))
        return copies

    mine = me // (n // 2)
    far = (1 - mine) * half
    near = mine * half
    halos = []
    for b, q in enumerate((1, 0, 3, 2)):
        for k in range(quarter):
            ins[q * quarter + k].wait()
        z = partner(q * quarter) // quarter
        copies = halo_copies(b, z * (nx // 4))
        for copy in copies:
            copy.start()
        halos += copies
    for copy in halos:
        copy.wait()

    def spans(lo, hi):
        out = []
        while lo < hi:
            size = min(2, hi - lo)
            out.append((PAD + 8 * lo, 8 * size))
            lo += size
        return out

    def before(i):
        return lax.rem(i + nx - 1, nx)

    def after(i):
        return lax.rem(i + 1, nx)

    def zp(x):
        return pltpu.roll(x, nz - 1, 1)

    def zm(x):
        return pltpu.roll(x, 1, 1)

    def beside(ref, i, r, size):
        c = ref[i, r : r + size, :]
        s = ref[before(i), r : r + size, :] + ref[after(i), r : r + size, :]
        y = ref[i, r - 1 : r - 1 + size, :] + ref[i, r + 1 : r + 1 + size, :]
        return c, s + y + (zp(c) + zm(c))

    def fold(x):
        t = x[0:8]
        for k in range(1, x.shape[0] // 8):
            t = t + x[8 * k : 8 * k + 8]
        u = t[:, 0:128]
        for k in range(1, nz // 128):
            u = u + t[:, 128 * k : 128 * k + 128]
        return u

    def over(lo, hi, body, acc=0, start=0, count=nx):
        def plane(i, acc):
            for r, size in spans(lo, hi):
                acc = body(i, r, size, acc)
            return acc
        return lax.fori_loop(start, start + count, plane, acc)

    own = (HY // 8, blocks - HY // 8)
    acc0 = jnp.zeros((8, 128), F32)

    def source(i, r, size):
        lower, upper = before(i), after(i)
        def at(k, q):
            return pv[k, r + q : r + q + size, :]
        c, cu, cd = at(i, 0), at(i, 1), at(i, -1)
        u, l = at(upper, 0), at(lower, 0)
        c2x = 2.0 * c
        xx = u + l - c2x
        yy = cu + cd - c2x
        zz = zp(c) + zm(c) - c2x
        xy = (at(upper, 1) - at(lower, 1)) - (at(upper, -1) - at(lower, -1))
        d = u - l
        xz = zp(d) - zm(d)
        g = cu - cd
        yz = zp(g) - zm(g)
        return xx * yy + (xx + yy) * zz - 0.0625 * (xy * xy + xz * xz + yz * yz)

    def source_plane(i, acc):
        for lo, hi in ((0, own[0]), own, (own[1], blocks)):
            for r, size in spans(lo, hi):
                s = source(i, r, size)
                fv[i, r : r + size, :] = -s
                if (lo, hi) == own:
                    acc = acc + fold(s)
        return acc

    sbuf[0] = lax.fori_loop(0, nx, source_plane, acc0)

    def share(buf, send, recv, k):
        return pltpu.make_async_remote_copy(
            buf.at[0], buf.at[k], send.at[k], recv.at[k],
            device_id={"gx": lax.rem(me + k, n)})

    def share_start(buf, send, recv):
        def go(k, _):
            share(buf, send, recv, k).start()
            return 0
        lax.fori_loop(1, n, go, 0)

    def share_wait(buf, send, recv):
        def go(k, _):
            share(buf, send, recv, k).wait()
            return 0
        lax.fori_loop(1, n, go, 0)
        return lax.fori_loop(1, n, lambda k, t: t + buf[k], buf[0])

    share_start(sbuf, s_send, s_recv)

    cr, cc = cf.shape[1:]
    batch = 4
    lanes = [(256 * k, 128 * k) for k in range(nz // 256)]
    slabs = range(nz // 128)
    wide = wv.at[:, PAD : PAD + cr, :]

    def restrict(lo, hi, residual):
        first, last = 4 * lo, 4 * hi
        def plane(j, _):
            for r, size in spans(lo, hi):
                x = residual(2 * j, r, size) + residual(2 * j + 1, r, size)
                for q in slabs:
                    tmp[q, r - PAD : r - PAD + size, :] = x[:, 128 * q : 128 * q + 128]
            span = last - first
            for q in slabs:
                x = tmp[q, pl.ds(2 * first, span, stride=2), :] + tmp[q, pl.ds(2 * first + 1, span, stride=2), :]
                wide[j, first:last, 128 * q : 128 * q + 128] = x * 0.125
            return 0
        lax.fori_loop(0, half, plane, 0)
        def lane_pairs(b, _):
            at = pl.ds(b * batch, batch)
            for fine, coarse in lanes:
                x = wide[at, :, fine : fine + 256].reshape(batch * cr, 256)
                cf[at, :, coarse : coarse + 128] = split_dot(x, rmat[...]).reshape(batch, cr, 128)
            return 0
        lax.fori_loop(0, half // batch, lane_pairs, 0)

    def residual_first(i, r, size):
        c, s = beside(fv, i, r, size)
        return c - A * (6.0 * c - s)

    restrict(0, blocks, residual_first)
    mean = jnp.sum(share_wait(sbuf, s_send, s_recv)) / cells

    def coarse_solve(shift):
        def first(j, _):
            f = (cf[j] + shift) * 4.0
            cf[j] = f
            ea[j] = A * f
            return 0
        lax.fori_loop(0, half, first, 0)
        src, dst = ea, eb
        for sweep in range(3):
            def again(j, _, src=src, dst=dst):
                v = src[j]
                s = src[lax.rem(j + half - 1, half)] + src[lax.rem(j + 1, half)]
                s = s + pltpu.roll(v, 1, 0) + pltpu.roll(v, cr - 1, 0)
                s = s + pltpu.roll(v, 1, 1) + pltpu.roll(v, cc - 1, 1)
                dst[j] = 0.2 * v + A * (cf[j] + s)
                return 0
            lax.fori_loop(0, half, again, 0)
            src, dst = dst, src
        return src

    def prolong(e, lo, hi, add):
        first, span = 4 * lo, 4 * (hi - lo)
        def lane_pairs(b, _):
            at = pl.ds(b * batch, batch)
            for fine, coarse in lanes:
                x = e[at, :, coarse : coarse + 128].reshape(batch * cr, 128)
                wide[at, :, fine : fine + 256] = split_dot(x, tmat[...]).reshape(batch, cr, 256)
            return 0
        lax.fori_loop(0, half // batch, lane_pairs, 0)
        def plane(j, _):
            for q in slabs:
                x = wide[j, first : first + span, 128 * q : 128 * q + 128]
                tmp[q, pl.ds(2 * first, span, stride=2), :] = x
                tmp[q, pl.ds(2 * first + 1, span, stride=2), :] = x
            for r, size in spans(lo, hi):
                x = jnp.concatenate([tmp[q, r - PAD : r - PAD + size, :] for q in slabs], axis=1)
                for q in range(2):
                    add(2 * j + q, r, size, x)
            return 0
        lax.fori_loop(0, half, plane, 0)

    def add_first(i, r, size, x):
        f = fv[i, r : r + size, :] + mean
        fv[i, r : r + size, :] = f
        pv[i, r : r + size, :] = A * f + x

    def add_second(i, r, size, x):
        pv[i, r : r + size, :] = pv[i, r : r + size, :] + x

    def relax(i, r, size, acc):
        c, s = beside(pv, i, r, size)
        wv[i, r : r + size, :] = 0.2 * c + A * (fv[i, r : r + size, :] + s)
        return acc

    def residual_of(ref, i, r, size):
        c, s = beside(ref, i, r, size)
        return c, fv[i, r : r + size, :] - (6.0 * c - s)

    def relax_norm(i, acc):
        for lo, hi in ((1, own[0]), own, (own[1], blocks - 1)):
            for r, size in spans(lo, hi):
                c, res = residual_of(wv, i, r, size)
                pv[i, r : r + size, :] = c + A * res
                if (lo, hi) == own:
                    acc = acc + fold(res * res)
        return acc

    prolong(coarse_solve(mean), 1, blocks - 1, add_first)
    over(1, blocks - 1, relax)
    nbuf[0, 0:8, :] = lax.fori_loop(0, nx, relax_norm, acc0)

    restrict(2, blocks - 2, lambda i, r, size: residual_of(pv, i, r, size)[1])
    prolong(coarse_solve(0.0), 2, blocks - 2, add_second)

    def out_copy(k):
        t = partner(k)
        src = wv.at[pl.ds(planes * t, planes), pl.ds(PAD + HY, rows), :]
        dst = o_ref.at[:, pl.ds(pl.multiple_of(here * rows, 8), rows), :]
        if k == 0:
            return pltpu.make_async_copy(src, dst, local_sem.at[1])
        return pltpu.make_async_remote_copy(
            src, dst, out_send.at[k], out_recv.at[k], device_id={"gx": t})

    outs = [out_copy(k) for k in range(n)]
    over(2, blocks - 2, relax, start=far, count=half)
    for k in range(n - 1, n // 2 - 1, -1):
        outs[k].start()
    over(2, blocks - 2, relax, start=near, count=half)
    for k in range(n // 2 - 1, -1, -1):
        outs[k].start()

    def norm_body(i, r, size, acc):
        res = residual_of(wv, i, r, size)[1]
        return acc + fold(res * res)

    nbuf[0, 8:16, :] = over(*own, norm_body, acc0)
    share_start(nbuf, n_send, n_recv)
    sums = share_wait(nbuf, n_send, n_recv)
    nrm_ref[0:8, :] = jnp.sqrt(jnp.full((8, 128), jnp.sum(sums[0:8]) / cells, F32))
    nrm_ref[8:16, :] = jnp.sqrt(jnp.full((8, 128), jnp.sum(sums[8:16]) / cells, F32))
    for copy in outs:
        copy.wait()


def on_device(n, potential):
    planes, ny, nz = potential.shape
    R = ny // n + 2 * HY
    nx = planes * n
    cr = (R // 2 + 7) // 8 * 8
    hops = -(-HY // (ny // n))
    fine = pltpu.VMEM((nx, R + 2 * PAD, nz), F32)
    small = pltpu.VMEM((nx // 2, cr, nz // 2), F32)
    dma = pltpu.SemaphoreType.DMA
    field, norms = pl.pallas_call(
        functools.partial(kernel, n),
        out_shape=(
            jax.ShapeDtypeStruct(potential.shape, F32),
            jax.ShapeDtypeStruct((16, 128), F32),
        ),
        in_specs=[pl.BlockSpec(memory_space=pl.ANY)],
        out_specs=(pl.BlockSpec(memory_space=pl.ANY), pl.BlockSpec(memory_space=pltpu.VMEM)),
        scratch_shapes=[
            fine, fine, fine, pltpu.VMEM((nz // 128, R, 128), F32), small, small, small,
            pltpu.VMEM((n, 8, 128), F32), pltpu.VMEM((n, 16, 128), F32),
            pltpu.VMEM((256, 128), BF16), pltpu.VMEM((128, 256), BF16),
            dma((n,)), dma((n,)), dma((4, 2, hops)), dma((4, 2, hops)),
            dma((n,)), dma((n,)), dma((n,)), dma((n,)), dma((n,)), dma((n,)), dma((2,)),
        ],
        compiler_params=pltpu.CompilerParams(
            collective_id=0, has_side_effects=True, vmem_limit_bytes=67043328),
        name="vcycles",
    )(potential)
    return field, jnp.stack([norms[0, 0], norms[8, 0]])


def solution(mesh):
    n = mesh.shape["gx"]
    return jax.shard_map(
        functools.partial(on_device, n),
        mesh=mesh,
        in_specs=P(("runs", "gx"), None, None),
        out_specs=(P(("runs", "gx"), None, None), P("runs")),
        check_vma=False,
    )
```

```python
import functools

import jax
import jax.numpy as jnp
from jax import lax
from jax.experimental import pallas as pl
from jax.experimental.pallas import tpu as pltpu
from jax.sharding import PartitionSpec as P

HY = 24
PAD = 8
A = 0.8 / 6.0
F32 = jnp.float32
BF16 = jnp.bfloat16


def split_dot(x, m):
    hi = x.astype(BF16)
    lo = (x - hi.astype(F32)).astype(BF16)
    return jnp.dot(hi, m, preferred_element_type=F32) + jnp.dot(lo, m, preferred_element_type=F32)


def loop(lo, count, body, acc, by):
    def some(h, acc):
        for q in range(by):
            acc = body(lo + by * h + q, acc)
        return acc
    return lax.fori_loop(0, count // by, some, acc)


def kernel(
    n, p_ref, o_ref, nrm_ref,
    pv, fv, wv, tmp, cf, ea, eb, sbuf, nbuf, rmat, tmat,
    in_send, in_recv, halo_send, halo_recv, s_send, s_recv, n_send, n_recv,
    out_send, out_recv, local_sem,
):
    planes, ny, nz = p_ref.shape
    rows = ny // n
    R = rows + 2 * HY
    blocks = R // 8
    nx = planes * n
    half = nx // 2
    cells = float(nx * ny * nz)
    chips = n // 2
    me = lax.axis_index("gx")

    def ring_of(d):
        chip = d // 2
        odd = chip % 2
        pos = (1 - odd) * (chip // 2) + odd * (chips - 1 - chip // 2)
        return 2 * pos + d % 2

    def device_at(r):
        pos = r // 2
        back = pos // (chips // 2)
        chip = (1 - back) * (2 * pos) + back * (2 * (chips - 1 - pos) + 1)
        return 2 * chip + r % 2

    def partner(k):
        t = 0
        bit = 1
        while bit < n:
            t = t + (((me // bit) % 2 + (k // bit) % 2) % 2) * bit
            bit *= 2
        return t

    here = ring_of(me)

    barrier = pltpu.get_barrier_semaphore()

    def greet(k, _):
        pl.semaphore_signal(barrier, inc=1, device_id={"gx": lax.rem(me + k, n)})
        return 0

    lax.fori_loop(1, n, greet, 0)
    pl.semaphore_wait(barrier, n - 1)

    def in_copy(k):
        t = partner(k)
        src = p_ref.at[:, pl.ds(pl.multiple_of(ring_of(t) * rows, 8), rows), :]
        dst = pv.at[pl.ds(planes * me, planes), pl.ds(PAD + HY, rows), :]
        if k == 0:
            return pltpu.make_async_copy(src, dst, local_sem.at[0])
        return pltpu.make_async_remote_copy(
            src, dst, in_send.at[k], in_recv.at[k], device_id={"gx": t})

    ins = [in_copy(k) for k in range(n)]
    quarter = n // 4
    for k in range(quarter):
        for q in (3, 1, 2, 0):
            ins[q * quarter + k].start()

    zeros = jnp.zeros((PAD, nz), F32)

    def clear(i, _):
        for ref in (pv, fv, wv):
            ref[i, 0:PAD, :] = zeros
            ref[i, PAD + R : 2 * PAD + R, :] = zeros
        return 0

    lax.fori_loop(0, nx, clear, 0)

    def pairs(shape, fine):
        idx = lax.broadcasted_iota(jnp.int32, shape, fine)
        other = lax.broadcasted_iota(jnp.int32, shape, 1 - fine)
        return jnp.where(idx // 2 == other, 1.0, 0.0).astype(BF16)

    rmat[...] = pairs(rmat.shape, 0)
    tmat[...] = pairs(tmat.shape, 1)

    def halo_copies(b, start):
        copies = []
        at = PAD + HY
        for h in range((HY + rows - 1) // rows):
            size = min(rows, HY - h * rows)
            span = pl.ds(start, nx // 4)
            copies.append(pltpu.make_async_remote_copy(
                pv.at[span, pl.ds(at + rows - size, size), :],
                pv.at[span, pl.ds(at - h * rows - size, size), :],
                halo_send.at[b, 0, h], halo_recv.at[b, 0, h],
                device_id={"gx": device_at((here + 1 + h) % n)}))
            copies.append(pltpu.make_async_remote_copy(
                pv.at[span, pl.ds(at, size), :],
                pv.at[span, pl.ds(at + rows + h * rows, size), :],
                halo_send.at[b, 1, h], halo_recv.at[b, 1, h],
                device_id={"gx": device_at((here + n - 1 - h) % n)}))
        return copies

    halos = []
    for b, q in enumerate((1, 0, 3, 2)):
        for k in range(quarter):
            ins[q * quarter + k].wait()
        z = partner(q * quarter) // quarter
        copies = halo_copies(b, z * (nx // 4))
        for copy in copies:
            copy.start()
        halos += copies
    for copy in halos:
        copy.wait()

    def spans(lo, hi):
        out = []
        while lo < hi:
            size = min(2, hi - lo)
            out.append((PAD + 8 * lo, 8 * size))
            lo += size
        return out

    def before(i):
        return lax.rem(i + nx - 1, nx)

    def after(i):
        return lax.rem(i + 1, nx)

    def zp(x):
        return pltpu.roll(x, nz - 1, 1)

    def zm(x):
        return pltpu.roll(x, 1, 1)

    def beside(ref, i, r, size):
        c = ref[i, r : r + size, :]
        s = ref[before(i), r : r + size, :] + ref[after(i), r : r + size, :]
        y = ref[i, r - 1 : r - 1 + size, :] + ref[i, r + 1 : r + 1 + size, :]
        return c, s + y + (zp(c) + zm(c))

    def fold(x):
        t = x[0:8]
        for k in range(1, x.shape[0] // 8):
            t = t + x[8 * k : 8 * k + 8]
        u = t[:, 0:128]
        for k in range(1, nz // 128):
            u = u + t[:, 128 * k : 128 * k + 128]
        return u

    def over(lo, hi, body, acc=0, start=0, count=nx):
        def plane(i, acc):
            for r, size in spans(lo, hi):
                acc = body(i, r, size, acc)
            return acc
        return loop(start, count, plane, acc, 4)

    own = (HY // 8, blocks - HY // 8)
    acc0 = jnp.zeros((8, 128), F32)

    def source(i, r, size):
        lower, upper = before(i), after(i)
        def at(k, q):
            return pv[k, r + q : r + q + size, :]
        c, cu, cd = at(i, 0), at(i, 1), at(i, -1)
        u, l = at(upper, 0), at(lower, 0)
        c2x = 2.0 * c
        xx = u + l - c2x
        yy = cu + cd - c2x
        zz = zp(c) + zm(c) - c2x
        xy = (at(upper, 1) - at(lower, 1)) - (at(upper, -1) - at(lower, -1))
        d = u - l
        xz = zp(d) - zm(d)
        g = cu - cd
        yz = zp(g) - zm(g)
        return xx * yy + (xx + yy) * zz - 0.0625 * (xy * xy + xz * xz + yz * yz)

    def source_plane(i, acc):
        for lo, hi in ((0, own[0]), own, (own[1], blocks)):
            for r, size in spans(lo, hi):
                s = source(i, r, size)
                fv[i, r : r + size, :] = -s
                if (lo, hi) == own:
                    acc = acc + fold(s)
        return acc

    sbuf[0] = loop(0, nx, source_plane, acc0, 2)

    def share(buf, send, recv, k):
        return pltpu.make_async_remote_copy(
            buf.at[0], buf.at[k], send.at[k], recv.at[k],
            device_id={"gx": lax.rem(me + k, n)})

    def share_start(buf, send, recv):
        def go(k, _):
            share(buf, send, recv, k).start()
            return 0
        lax.fori_loop(1, n, go, 0)

    def share_wait(buf, send, recv):
        def go(k, _):
            share(buf, send, recv, k).wait()
            return 0
        lax.fori_loop(1, n, go, 0)
        return lax.fori_loop(1, n, lambda k, t: t + buf[k], buf[0])

    share_start(sbuf, s_send, s_recv)

    cr, cc = cf.shape[1:]
    batch = 8
    lanes = [(256 * k, 128 * k) for k in range(nz // 256)]
    slabs_n = nz // 128
    slabs = range(slabs_n)
    wide = wv.at[:, PAD : PAD + cr, :]

    def restrict(lo, hi, residual):
        first, last = 4 * lo, 4 * hi
        def plane(j, _, z):
            for r, size in spans(lo, hi):
                x = residual(2 * j, r, size) + residual(2 * j + 1, r, size)
                for q in slabs:
                    tmp[z + q, r - PAD : r - PAD + size, :] = x[:, 128 * q : 128 * q + 128]
            span = last - first
            for q in slabs:
                x = tmp[z + q, pl.ds(2 * first, span, stride=2), :] + tmp[z + q, pl.ds(2 * first + 1, span, stride=2), :]
                wide[j, first:last, 128 * q : 128 * q + 128] = x * 0.125
            return 0
        lax.fori_loop(0, half // 2, lambda h, a: plane(2 * h + 1, plane(2 * h, a, 0), slabs_n), 0)
        def lane_pairs(b, _):
            at = pl.ds(b * batch, batch)
            for fine, coarse in lanes:
                x = wide[at, :, fine : fine + 256].reshape(batch * cr, 256)
                cf[at, :, coarse : coarse + 128] = split_dot(x, rmat[...]).reshape(batch, cr, 128)
            return 0
        lax.fori_loop(0, half // batch, lane_pairs, 0)

    def residual_first(i, r, size):
        c, s = beside(fv, i, r, size)
        return c - A * (6.0 * c - s)

    restrict(0, blocks, residual_first)
    mean = jnp.sum(share_wait(sbuf, s_send, s_recv)) / cells

    def coarse_solve(shift):
        def first(j, _):
            f = (cf[j] + shift) * 4.0
            cf[j] = f
            ea[j] = A * f
            return 0
        loop(0, half, first, 0, 4)
        src, dst = ea, eb
        for sweep in range(3):
            def again(j, _, src=src, dst=dst):
                v = src[j]
                s = src[lax.rem(j + half - 1, half)] + src[lax.rem(j + 1, half)]
                s = s + pltpu.roll(v, 1, 0) + pltpu.roll(v, cr - 1, 0)
                s = s + pltpu.roll(v, 1, 1) + pltpu.roll(v, cc - 1, 1)
                dst[j] = 0.2 * v + A * (cf[j] + s)
                return 0
            loop(0, half, again, 0, 4)
            src, dst = dst, src
        return src

    def prolong(e, lo, hi, add):
        first, span = 4 * lo, 4 * (hi - lo)
        def lane_pairs(b, _):
            at = pl.ds(b * batch, batch)
            for fine, coarse in lanes:
                x = e[at, :, coarse : coarse + 128].reshape(batch * cr, 128)
                wide[at, :, fine : fine + 256] = split_dot(x, tmat[...]).reshape(batch, cr, 256)
            return 0
        lax.fori_loop(0, half // batch, lane_pairs, 0)
        def plane(j, _, z):
            for q in slabs:
                x = wide[j, first : first + span, 128 * q : 128 * q + 128]
                tmp[z + q, pl.ds(2 * first, span, stride=2), :] = x
                tmp[z + q, pl.ds(2 * first + 1, span, stride=2), :] = x
            for r, size in spans(lo, hi):
                x = jnp.concatenate([tmp[z + q, r - PAD : r - PAD + size, :] for q in slabs], axis=1)
                for q in range(2):
                    add(2 * j + q, r, size, x)
            return 0
        lax.fori_loop(0, half // 2, lambda h, a: plane(2 * h + 1, plane(2 * h, a, 0), slabs_n), 0)

    def add_first(i, r, size, x):
        f = fv[i, r : r + size, :] + mean
        fv[i, r : r + size, :] = f
        pv[i, r : r + size, :] = A * f + x

    def add_second(i, r, size, x):
        pv[i, r : r + size, :] = pv[i, r : r + size, :] + x

    def relax(i, r, size, acc):
        c, s = beside(pv, i, r, size)
        wv[i, r : r + size, :] = 0.2 * c + A * (fv[i, r : r + size, :] + s)
        return acc

    def residual_of(ref, i, r, size):
        c, s = beside(ref, i, r, size)
        return c, fv[i, r : r + size, :] - (6.0 * c - s)

    def relax_norm(i, acc):
        for lo, hi in ((1, own[0]), own, (own[1], blocks - 1)):
            for r, size in spans(lo, hi):
                c, res = residual_of(wv, i, r, size)
                pv[i, r : r + size, :] = c + A * res
                if (lo, hi) == own:
                    acc = acc + fold(res * res)
        return acc

    prolong(coarse_solve(mean), 1, blocks - 1, add_first)
    over(1, blocks - 1, relax)
    nbuf[0, 0:8, :] = loop(0, nx, relax_norm, acc0, 4)

    restrict(2, blocks - 2, lambda i, r, size: residual_of(pv, i, r, size)[1])
    prolong(coarse_solve(0.0), 2, blocks - 2, add_second)

    def out_copy(k):
        t = partner(k)
        src = wv.at[pl.ds(planes * t, planes), pl.ds(PAD + HY, rows), :]
        dst = o_ref.at[:, pl.ds(pl.multiple_of(here * rows, 8), rows), :]
        if k == 0:
            return pltpu.make_async_copy(src, dst, local_sem.at[1])
        return pltpu.make_async_remote_copy(
            src, dst, out_send.at[k], out_recv.at[k], device_id={"gx": t})

    outs = [out_copy(k) for k in range(n)]
    for q in (3, 2, 1, 0):
        z = partner(q * quarter) // quarter
        over(2, blocks - 2, relax, start=z * (nx // 4), count=nx // 4)
        for k in range(quarter):
            outs[q * quarter + k].start()

    def norm_body(i, r, size, acc):
        res = residual_of(wv, i, r, size)[1]
        return acc + fold(res * res)

    nbuf[0, 8:16, :] = over(*own, norm_body, acc0)
    share_start(nbuf, n_send, n_recv)
    sums = share_wait(nbuf, n_send, n_recv)
    nrm_ref[0:8, :] = jnp.sqrt(jnp.full((8, 128), jnp.sum(sums[0:8]) / cells, F32))
    nrm_ref[8:16, :] = jnp.sqrt(jnp.full((8, 128), jnp.sum(sums[8:16]) / cells, F32))
    for copy in outs:
        copy.wait()


def on_device(n, potential):
    planes, ny, nz = potential.shape
    R = ny // n + 2 * HY
    nx = planes * n
    cr = (R // 2 + 7) // 8 * 8
    hops = -(-HY // (ny // n))
    fine = pltpu.VMEM((nx, R + 2 * PAD, nz), F32)
    small = pltpu.VMEM((nx // 2, cr, nz // 2), F32)
    dma = pltpu.SemaphoreType.DMA
    field, norms = pl.pallas_call(
        functools.partial(kernel, n),
        out_shape=(
            jax.ShapeDtypeStruct(potential.shape, F32),
            jax.ShapeDtypeStruct((16, 128), F32),
        ),
        in_specs=[pl.BlockSpec(memory_space=pl.ANY)],
        out_specs=(pl.BlockSpec(memory_space=pl.ANY), pl.BlockSpec(memory_space=pltpu.VMEM)),
        scratch_shapes=[
            fine, fine, fine, pltpu.VMEM((2 * nz // 128, R, 128), F32), small, small, small,
            pltpu.VMEM((n, 8, 128), F32), pltpu.VMEM((n, 16, 128), F32),
            pltpu.VMEM((256, 128), BF16), pltpu.VMEM((128, 256), BF16),
            dma((n,)), dma((n,)), dma((4, 2, hops)), dma((4, 2, hops)),
            dma((n,)), dma((n,)), dma((n,)), dma((n,)), dma((n,)), dma((n,)), dma((2,)),
        ],
        compiler_params=pltpu.CompilerParams(
            collective_id=0, has_side_effects=True, vmem_limit_bytes=67043328),
        name="vcycles",
    )(potential)
    return field, jnp.stack([norms[0, 0], norms[8, 0]])


def solution(mesh):
    n = mesh.shape["gx"]
    return jax.shard_map(
        functools.partial(on_device, n),
        mesh=mesh,
        in_specs=P(("runs", "gx"), None, None),
        out_specs=(P(("runs", "gx"), None, None), P("runs")),
        check_vma=False,
    )
```
